256 devices in a mesh: fsdp: 64 (over x, z, core), rep: 4 (over y).
Axes of the slice: x: 4, y: 4, z: 8, core: 2. Of those that a mesh axis runs over, the one named last changes fastest.
Arguments:
- grad: bfloat16 [128, 256, 2048], P(None, 'fsdp'), may hold values from -6 to 6
- momentum: float32 [128, 256, 2048], P(None, 'fsdp'), may hold values from -6 to 6
- owner_list: int32 [128], replicated, may hold values from 0 to 63, as said below
Outputs:
- new_momentum: float32 [128, 256, 2048], P(None, 'fsdp')
- update: bfloat16 [128, 256, 2048], P(None, 'fsdp')
- owned_update: bfloat16 [256, 256, 2048], P(('fsdp', 'rep'))
The draws below stay inside these ranges and needn't reach their ends.
Inputs may be any that keep to these rules, and one draw needn't show every extreme that they name: `owner_list`: no owner is named by more than 4 matrices; some owner is named by exactly 4 in every draw.
All inputs are finite; a program needn't handle non-finite values.
Results may differ from the reference program's by a relative error of at most 0.03.
Values may be sent and summed in bfloat16 or wider, within the bound.
A program may use at most 128 MiB of HBM per device.

```python
import jax
import jax.numpy as jnp
from jax import lax

ROWS = 256
COLS = 2048
CAP = 4
ITERS = 5
MATS = 128
N_FSDP = 64


def draw_owner_list(key, part):
    first_key, second_key, third_key = jax.random.split(jax.random.fold_in(key, 17), 3)
    order = jax.random.permutation(first_key, N_FSDP)
    halves = jax.random.randint(second_key, (N_FSDP // 2,), 0, CAP + 1).astype(jnp.int32)
    halves = halves.at[0].set(CAP)
    ordered_counts = jnp.stack([halves, CAP - halves], axis=1).reshape(-1).astype(jnp.int32)
    counts = jnp.zeros((N_FSDP,), jnp.int32).at[order].set(ordered_counts)
    ends = jnp.cumsum(counts)
    grouped = jnp.searchsorted(ends, jnp.arange(MATS), side='right').astype(jnp.int32)
    return grouped[jax.random.permutation(third_key, MATS)]


def shard_levels(own_key, extent, cuts, smallest, largest):
    level = 1.0
    for dim, blocks in cuts:
        draws = jax.random.uniform(jax.random.fold_in(jax.random.fold_in(own_key, 6), dim), (blocks,), jnp.float32, smallest / len(cuts), largest / len(cuts))
        level = level * jnp.repeat(jnp.exp(draws), extent[dim] // blocks).reshape((-1,) + (1,) * (len(extent) - 1 - dim))
    return level


def noise(rng, shape, spread, limit, pieces=(), kind=jnp.bfloat16):
    loudness = shard_levels(rng, shape, pieces, -0.22, 0.18) if pieces else 1.0
    result = jax.random.normal(rng, shape, jnp.float32) * spread * loudness
    return jnp.minimum(jnp.maximum(result, -limit), limit).astype(kind)


def setup_inputs(seed: int = 0) -> dict:
    seeds = jax.random.split(jax.random.key(seed), 4)
    grad = noise(seeds[0], (MATS, ROWS, COLS), 1.0, 6.0, ((1, 64),))
    momentum = noise(seeds[1], (MATS, ROWS, COLS), 1.0, 6.0, ((1, 64),), jnp.float32)
    owner_list = draw_owner_list(jax.random.fold_in(seeds[3], 71), 0)
    return dict(grad=grad, momentum=momentum, owner_list=owner_list)


decay_rate = 0.95
norm_eps = 1e-07
quintic_a = 3.4445
quintic_b = -4.775
quintic_c = 2.0315

def newton(blended):
    values = blended.astype(jnp.float32)
    total = jnp.sqrt(jnp.sum(values * values))
    current = (values / (total + norm_eps)).astype(jnp.bfloat16)
    for iteration in range(ITERS):
        gram = jnp.dot(current, current.T, preferred_element_type=jnp.float32).astype(jnp.bfloat16)
        square = jnp.dot(gram, gram, preferred_element_type=jnp.float32)
        poly = (quintic_b * gram.astype(jnp.float32) + quintic_c * square).astype(jnp.bfloat16)
        applied = jnp.dot(poly, current, preferred_element_type=jnp.float32)
        current = (quintic_a * current.astype(jnp.float32) + applied).astype(jnp.bfloat16)
    return current

def reference(grad, momentum, owner_list):
    new_momentum = decay_rate * momentum + grad.astype(jnp.float32)
    blended = (grad.astype(jnp.float32) + decay_rate * new_momentum).astype(jnp.bfloat16)
    update = lax.map(newton, blended)
    order = jnp.arange(MATS)
    earlier = order[None, :] < order[:, None]
    same_owner = owner_list[None, :] == owner_list[:, None]
    slot_index = lax.optimization_barrier(jnp.sum(jnp.logical_and(earlier, same_owner), axis=1)).astype(jnp.int32)
    position = (owner_list * CAP + slot_index).astype(jnp.int32)
    owned_update = jnp.zeros((N_FSDP * CAP, ROWS, COLS), jnp.bfloat16).at[position].set(update)
    return (new_momentum, update, owned_update)
```

```python
import functools

import jax
import jax.numpy as jnp
from jax import lax
from jax.experimental import pallas as pl
from jax.experimental.pallas import tpu as pltpu
from jax.sharding import PartitionSpec as P

ITERS = 5
decay_rate = 0.95
norm_eps = 1e-07
quintic_a = 3.4445
quintic_b = -4.775
quintic_c = 2.0315

MESH = pl.DeviceIdType.MESH
NX, NZ, NY = 4, 8, 4
CHIPS = NX * NZ
OWNERS = 2 * CHIPS
MATS = 128


def routing(owner_list, plane, me):
    order = jnp.arange(MATS, dtype=jnp.int32)
    owner = owner_list
    before = order[None, :] < order[:, None]
    slot = jnp.sum(before & (owner[None, :] == owner[:, None]), axis=1, dtype=jnp.int32)
    cell_slot = order // CHIPS
    cell_owner = (order % CHIPS) * 2 + cell_slot // 2
    code = owner * 4 + slot
    cell_code = cell_owner * 4 + cell_slot
    match = code[None, :] == cell_code[:, None]
    filled = jnp.any(match, axis=1)
    in_cell = (slot // 2) == (owner % 2)
    spare_rank = jnp.sum(before & ~in_cell[None, :], axis=1, dtype=jnp.int32)
    empty_rank = jnp.sum(before & ~filled[None, :], axis=1, dtype=jnp.int32)
    stand_in = (spare_rank[None, :] == empty_rank[:, None]) & ~filled[:, None] & ~in_cell[None, :]
    computed = match | stand_in
    cell_of = jnp.sum(jnp.where(computed, order[:, None], 0), axis=0, dtype=jnp.int32)
    chip = jnp.arange(CHIPS, dtype=jnp.int32)
    core = plane // 2
    wanted = cell_of[None, :] == (plane * CHIPS + chip)[:, None]
    to_cells = jnp.sum(jnp.where(wanted, order[None, :], 0), axis=1, dtype=jnp.int32)
    other = code[None, :] == ((chip * 2 + 1 - core) * 4 + plane)[:, None]
    to_others = jnp.sum(jnp.where(other, order[None, :], 0), axis=1, dtype=jnp.int32)
    own = jnp.any(code == me * 4 + plane).astype(jnp.int32)
    return jnp.concatenate([to_cells, to_others, cell_of, own[None]])


def kernel(table, grad_hbm, momentum_hbm, new_ref, update_ref, owned_ref, grad, momentum, staged, x_ref, cells,
           in_sem, send_sem, recv_sem, self_sem, back_send, back_recv, rep_send, rep_recv):
    f = lax.axis_index("fsdp")
    y = lax.axis_index("rep")
    chip = f // 2
    core = f % 2
    px = chip // NZ
    pz = chip % NZ
    cell_core = y // 2
    is_cell = core == cell_core

    load_grad = pltpu.make_async_copy(grad_hbm, grad, in_sem.at[0])
    load_momentum = pltpu.make_async_copy(momentum_hbm, momentum, in_sem.at[1])
    load_grad.start()
    load_momentum.start()

    barrier = pltpu.get_barrier_semaphore()

    @pl.loop(1, OWNERS)
    def _(k):
        pl.semaphore_signal(barrier, inc=1, device_id={"fsdp": lax.rem(f + k, OWNERS)}, device_id_type=MESH)

    for k in range(1, NY):
        pl.semaphore_signal(barrier, inc=1, device_id={"rep": lax.rem(y + k, NY)}, device_id_type=MESH)
    load_grad.wait()
    load_momentum.wait()
    pl.semaphore_wait(barrier, OWNERS - 1 + NY - 1)

    def chip_at(j):
        return lax.rem(px + j // NZ, NX) * NZ + lax.rem(pz + lax.rem(j, NZ), NZ)

    def stage(there, part):
        which = table[part * CHIPS + there]
        g = grad[which].astype(jnp.float32)
        blended = g + decay_rate * (decay_rate * momentum[which] + g)
        staged[part * CHIPS + there] = blended.astype(jnp.bfloat16)

    def send(there, part, to):
        pltpu.make_async_remote_copy(
            src_ref=staged.at[part * CHIPS + there],
            dst_ref=x_ref.at[pl.ds(f * 4, 4)],
            send_sem=send_sem,
            recv_sem=recv_sem,
            device_id={"fsdp": to},
            device_id_type=MESH,
        ).start()

    for part in range(2):
        to_core = cell_core if part == 0 else 1 - cell_core
        stage(chip, part)

        @pl.when(core == to_core)
        def _():
            pltpu.make_async_copy(staged.at[part * CHIPS + chip], x_ref.at[pl.ds(f * 4, 4)], self_sem.at[0]).start()

        @pl.when(core != to_core)
        def _():
            send(chip, part, chip * 2 + to_core)

        @pl.loop(1, CHIPS)
        def _(j):
            there = chip_at(j)
            stage(there, part)
            send(there, part, there * 2 + to_core)

    @pl.loop(0, MATS)
    def _(m):
        new_ref[m] = decay_rate * momentum[m] + grad[m].astype(jnp.float32)

    def receive():
        pltpu.make_async_copy(staged.at[0], x_ref.at[pl.ds(f * 4, 4)], self_sem.at[0]).wait()
        half = staged.at[pl.ds(0, OWNERS - 1)]
        pltpu.make_async_copy(half, half, recv_sem).wait()

    def newton():
        def gram_of(x):
            return lax.dot_general(x, x, (((1,), (1,)), ((), ())), preferred_element_type=jnp.float32)

        def poly_of(gram):
            low = gram.astype(jnp.bfloat16)
            square = jnp.dot(low, low, preferred_element_type=jnp.float32)
            return (quintic_b * low.astype(jnp.float32) + quintic_c * square).astype(jnp.bfloat16)

        def apply(poly, scale):
            for c in range(4):
                cols = pl.ds(c * 512, 512)
                x = x_ref[:, cols]
                applied = jnp.dot(poly, x, preferred_element_type=jnp.float32)
                y_new = quintic_a * x.astype(jnp.float32) + applied
                if scale is not None:
                    y_new = y_new * scale
                x_ref[:, cols] = y_new.astype(jnp.bfloat16)

        gram = gram_of(x_ref[...])
        row = lax.broadcasted_iota(jnp.int32, gram.shape, 0)
        col = lax.broadcasted_iota(jnp.int32, gram.shape, 1)
        total = jnp.sum(jnp.where(row == col, gram, 0.0), axis=(0, 1), keepdims=True)
        scale = 1.0 / (jnp.sqrt(total) + norm_eps)
        apply(poly_of(gram * (scale * scale)), scale)

        @pl.loop(1, ITERS)
        def _(i):
            apply(poly_of(gram_of(x_ref[...])), None)

    def back_arrival(j):
        here = y * CHIPS + lax.rem(px + NX - j // NZ, NX) * NZ + lax.rem(pz + NZ - lax.rem(j, NZ), NZ)
        return here

    @pl.when(is_cell)
    def _():
        receive()
        newton()
        mine = cells.at[y * CHIPS + chip]

        def give_back(j, there, to_core):
            pltpu.make_async_remote_copy(
                src_ref=x_ref.at[pl.ds((there * 2 + to_core) * 4, 4)],
                dst_ref=mine,
                send_sem=back_send,
                recv_sem=back_recv.at[j],
                device_id={"fsdp": there * 2 + to_core},
                device_id_type=MESH,
            ).start()

        pltpu.make_async_copy(x_ref.at[pl.ds(f * 4, 4)], mine, back_recv.at[0]).start()
        give_back(0, chip, 1 - core)

        @pl.loop(1, CHIPS)
        def _(j):
            there = chip_at(j)
            give_back(j, there, 0)
            give_back(j, there, 1)

    @pl.loop(0, CHIPS)
    def _(j):
        here = cells.at[back_arrival(j)]
        pltpu.make_async_copy(here, here, back_recv.at[j]).wait()
        for k in range(1, NY):
            pltpu.make_async_remote_copy(
                src_ref=here,
                dst_ref=here,
                send_sem=rep_send,
                recv_sem=rep_recv.at[k - 1],
                device_id={"rep": lax.rem(y + k, NY)},
                device_id_type=MESH,
            ).start()

    @pl.when(jnp.logical_not(is_cell))
    def _():
        receive()
        newton()

    keep = table[2 * CHIPS + MATS] != 0
    owned_ref[...] = jnp.where(keep, x_ref[...], jnp.zeros(x_ref.shape, x_ref.dtype))

    plane_cells = cells.at[pl.ds(0, CHIPS)]
    for k in range(1, NY):
        pltpu.make_async_copy(plane_cells, plane_cells, rep_recv.at[k - 1]).wait()

    @pl.loop(0, MATS)
    def _(m):
        update_ref[m] = cells[table[2 * CHIPS + m]]

    most = staged.at[pl.ds(0, OWNERS - 1)]
    pltpu.make_async_copy(most, most, send_sem).wait()

    @pl.when(is_cell)
    def _():
        pltpu.make_async_copy(most, most, back_send).wait()

    sent = cells.at[pl.ds(0, 3 * CHIPS)]
    pltpu.make_async_copy(sent, sent, rep_send).wait()


def local(grad, momentum, owner_list):
    mats, rows, cols = grad.shape
    me = lax.axis_index("fsdp")
    table = routing(owner_list, lax.axis_index("rep"), me)
    vmem = pl.BlockSpec(memory_space=pltpu.VMEM)
    hbm = pl.BlockSpec(memory_space=pl.ANY)
    dma = pltpu.SemaphoreType.DMA
    new_momentum, update, owned = pl.pallas_call(
        kernel,
        out_shape=(
            jax.ShapeDtypeStruct(momentum.shape, jnp.float32),
            jax.ShapeDtypeStruct(grad.shape, jnp.bfloat16),
            jax.ShapeDtypeStruct((rows * OWNERS, cols), jnp.bfloat16),
        ),
        in_specs=[pl.BlockSpec(memory_space=pltpu.SMEM), hbm, hbm],
        out_specs=(vmem, vmem, vmem),
        scratch_shapes=[
            pltpu.VMEM((mats, rows, cols), jnp.bfloat16),
            pltpu.VMEM((mats, rows, cols), jnp.float32),
            pltpu.VMEM((OWNERS, rows, cols), jnp.bfloat16),
            pltpu.VMEM((rows * OWNERS, cols), jnp.bfloat16),
            pltpu.VMEM((mats, rows, cols), jnp.bfloat16),
            dma((2,)),
            dma,
            dma,
            dma((1,)),
            dma,
            dma((CHIPS,)),
            dma,
            dma((NY - 1,)),
        ],
        compiler_params=pltpu.CompilerParams(
            collective_id=0, has_side_effects=True, vmem_limit_bytes=40 * 1024 * 1024
        ),
        name="muon",
    )(table, grad, momentum)
    return new_momentum, update, owned[None]


def solution(mesh):
    in_specs = (P(None, "fsdp", None), P(None, "fsdp", None), P())
    out_specs = (P(None, "fsdp", None), P(None, "fsdp", None), P(("fsdp", "rep"), None, None))
    return jax.shard_map(local, mesh=mesh, in_specs=in_specs, out_specs=out_specs, check_vma=False)
```

```python
import functools

import jax
import jax.numpy as jnp
from jax import lax
from jax.experimental import pallas as pl
from jax.experimental.pallas import tpu as pltpu
from jax.sharding import PartitionSpec as P

ITERS = 5
decay_rate = 0.95
norm_eps = 1e-07
quintic_a = 3.4445
quintic_b = -4.775
quintic_c = 2.0315

MESH = pl.DeviceIdType.MESH
NX, NZ, NY = 4, 8, 4
CHIPS = NX * NZ
OWNERS = 2 * CHIPS
MATS = 128
BLOCK = 4
BLOCKS = CHIPS // BLOCK
LAG = 2
FIRST_STEP = 2


def routing(owner_row, table, plane, me):
    square = (MATS, MATS)
    down = lax.broadcasted_iota(jnp.int32, square, 0)
    along = lax.broadcasted_iota(jnp.int32, square, 1)
    owner_r = jnp.broadcast_to(owner_row, square)
    owner_c = owner_r.T
    same = jnp.where(owner_r == owner_c, 1, 0)
    slot_r = jnp.sum(jnp.where(down < along, same, 0), axis=0, keepdims=True)
    slot_c = jnp.sum(jnp.where(along < down, same, 0), axis=1, keepdims=True)
    code_r = owner_r * 4 + slot_r
    code_c = owner_c * 4 + slot_c

    def cell_code(q):
        slot = q // CHIPS
        return ((q % CHIPS) * 2 + slot // 2) * 4 + slot

    def spare(owner, slot):
        return jnp.where((slot // 2) == (owner % 2), 0, 1)

    spare_r = spare(owner_r, slot_r)
    spare_c = spare(owner_c, slot_c)
    match = jnp.where(code_r == cell_code(down), 1, 0)
    empty_c = 1 - jnp.max(match, axis=1, keepdims=True)
    empty_r = 1 - jnp.max(jnp.where(code_c == cell_code(along), 1, 0), axis=0, keepdims=True)
    spare_rank = jnp.sum(jnp.where(down < along, spare_c, 0), axis=0, keepdims=True)
    empty_rank = jnp.sum(jnp.where(along < down, jnp.broadcast_to(empty_r, square), 0), axis=1, keepdims=True)
    stand_in = jnp.where(spare_rank == empty_rank, spare_r * empty_c, 0)
    cell_of = jnp.sum((match + stand_in) * down, axis=0, keepdims=True)
    cell_of_c = jnp.broadcast_to(cell_of, square).T
    other = ((along - CHIPS) * 2 + 1 - plane // 2) * 4 + plane
    wanted = jnp.where(along < 2 * CHIPS, other, me * 4 + plane)
    hit = jnp.where(along < CHIPS, cell_of_c - plane * CHIPS - along, code_c - wanted) == 0
    number = jnp.where(along < 2 * CHIPS, down, 1)
    table[0:1, :] = jnp.clip(jnp.sum(jnp.where(hit, number, 0), axis=0, keepdims=True), 0, MATS - 1)
    table[1:2, :] = jnp.clip(cell_of, 0, MATS - 1)


def kernel(owner_ref, grad_hbm, momentum_hbm, new_ref, cells, owned_ref, table_ref, grad, momentum, staged, x_ref, table,
           in_sem, send_sem, recv_sem, self_sem, back_send, back_recv, rep_send, up_recv, down_recv, far_recv):
    f = lax.axis_index("fsdp")
    y = lax.axis_index("rep")
    chip = f // 2
    core = f % 2
    px = chip // NZ
    pz = chip % NZ
    cell_core = y // 2
    is_cell = core == cell_core

    load_grad = pltpu.make_async_copy(grad_hbm, grad, in_sem.at[0])
    load_momentum = pltpu.make_async_copy(momentum_hbm, momentum, in_sem.at[1])
    load_grad.start()
    load_momentum.start()

    barrier = pltpu.get_barrier_semaphore()

    @pl.loop(1, OWNERS)
    def _(k):
        pl.semaphore_signal(barrier, inc=1, device_id={"fsdp": lax.rem(f + k, OWNERS)}, device_id_type=MESH)

    for k in range(1, NY):
        pl.semaphore_signal(barrier, inc=1, device_id={"rep": lax.rem(y + k, NY)}, device_id_type=MESH)
    routing(owner_ref[...], table_ref, y, f)
    load_table = pltpu.make_async_copy(table_ref, table, in_sem.at[2])
    load_table.start()
    load_table.wait()
    load_grad.wait()
    load_momentum.wait()
    pl.semaphore_wait(barrier, OWNERS - 1 + NY - 1)

    def chip_at(j):
        return lax.rem(px + j // NZ, NX) * NZ + lax.rem(pz + lax.rem(j, NZ), NZ)

    def stage(there, part):
        which = table[0, part * CHIPS + there]
        g = grad[which].astype(jnp.float32)
        blended = g + decay_rate * (decay_rate * momentum[which] + g)
        staged[part * CHIPS + there] = blended.astype(jnp.bfloat16)

    def send(there, part, to):
        pltpu.make_async_remote_copy(
            src_ref=staged.at[part * CHIPS + there],
            dst_ref=x_ref.at[pl.ds(f * 4, 4)],
            send_sem=send_sem,
            recv_sem=recv_sem,
            device_id={"fsdp": to},
            device_id_type=MESH,
        ).start()

    for part in range(2):
        to_core = cell_core if part == 0 else 1 - cell_core
        stage(chip, part)

        @pl.when(core == to_core)
        def _():
            pltpu.make_async_copy(staged.at[part * CHIPS + chip], x_ref.at[pl.ds(f * 4, 4)], self_sem.at[0]).start()

        @pl.when(core != to_core)
        def _():
            send(chip, part, chip * 2 + to_core)

        @pl.loop(1, CHIPS)
        def _(j):
            there = chip_at(j)
            stage(there, part)
            send(there, part, there * 2 + to_core)

    @pl.loop(0, MATS)
    def _(m):
        new_ref[m] = decay_rate * momentum[m] + grad[m].astype(jnp.float32)

    def receive():
        pltpu.make_async_copy(staged.at[0], x_ref.at[pl.ds(f * 4, 4)], self_sem.at[0]).wait()
        half = staged.at[pl.ds(0, OWNERS - 1)]
        pltpu.make_async_copy(half, half, recv_sem).wait()

    def newton_step(first):
        x = x_ref[...]
        gram = lax.dot_general(x, x, (((1,), (1,)), ((), ())), preferred_element_type=jnp.float32)
        if first:
            row = lax.broadcasted_iota(jnp.int32, gram.shape, 0)
            col = lax.broadcasted_iota(jnp.int32, gram.shape, 1)
            total = jnp.sum(jnp.where(row == col, gram, 0.0), axis=(0, 1), keepdims=True)
            scale = 1.0 / (jnp.sqrt(total) + norm_eps)
            gram = gram * (scale * scale)
        low = gram.astype(jnp.bfloat16)
        square = jnp.dot(low, low, preferred_element_type=jnp.float32)
        poly = (quintic_b * low.astype(jnp.float32) + quintic_c * square).astype(jnp.bfloat16)
        for c in range(4):
            cols = pl.ds(c * 512, 512)
            part = x_ref[:, cols]
            result = quintic_a * part.astype(jnp.float32) + jnp.dot(poly, part, preferred_element_type=jnp.float32)
            if first:
                result = result * scale
            x_ref[:, cols] = result.astype(jnp.bfloat16)

    def back_chip(j):
        return lax.rem(px + NX - j // NZ, NX) * NZ + lax.rem(pz + NZ - lax.rem(j, NZ), NZ)

    up = lax.rem(y + 1, NY)
    below = lax.rem(y + NY - 1, NY)

    @pl.when(is_cell)
    def _():
        receive()
        newton_step(True)

        @pl.loop(1, ITERS)
        def _(i):
            newton_step(False)

        mine = cells.at[y * CHIPS + chip]

        def give_back(j, there, to_core):
            pltpu.make_async_remote_copy(
                src_ref=x_ref.at[pl.ds((there * 2 + to_core) * 4, 4)],
                dst_ref=mine,
                send_sem=back_send,
                recv_sem=back_recv.at[j],
                device_id={"fsdp": there * 2 + to_core},
                device_id_type=MESH,
            ).start()

        pltpu.make_async_copy(x_ref.at[pl.ds(f * 4, 4)], mine, back_recv.at[0]).start()
        give_back(0, chip, 1 - core)

        @pl.loop(1, CHIPS)
        def _(j):
            there = chip_at(j)
            give_back(j, there, 0)
            give_back(j, there, 1)

    def rep_copy(unit, to, sem):
        here = cells.at[unit]
        return pltpu.make_async_remote_copy(
            src_ref=here, dst_ref=here, send_sem=rep_send, recv_sem=sem, device_id={"rep": to}, device_id_type=MESH
        )

    def own(j):
        unit = y * CHIPS + back_chip(j)
        pltpu.make_async_copy(cells.at[unit], cells.at[unit], back_recv.at[j]).wait()
        rep_copy(unit, up, up_recv.at[j]).start()
        rep_copy(unit, below, down_recv.at[j]).start()

    def onward(j):
        unit = below * CHIPS + back_chip(j)
        pltpu.make_async_copy(cells.at[unit], cells.at[unit], up_recv.at[j]).wait()
        rep_copy(unit, up, far_recv).start()
        unit = up * CHIPS + back_chip(j + 1)
        pltpu.make_async_copy(cells.at[unit], cells.at[unit], down_recv.at[j + 1]).wait()
        rep_copy(unit, below, far_recv).start()

    @pl.loop(0, BLOCKS + LAG)
    def _(b):
        @pl.when(b < BLOCKS)
        def _():
            @pl.loop(0, BLOCK)
            def _(i):
                own(b * BLOCK + i)

        @pl.when(b >= LAG)
        def _():
            @pl.loop(0, BLOCK // 2)
            def _(i):
                onward((b - LAG) * BLOCK + 2 * i)

        step = b - FIRST_STEP

        @pl.when(jnp.logical_and(jnp.logical_not(is_cell), step == 0))
        def _():
            receive()
            newton_step(True)

        @pl.when(jnp.logical_and(jnp.logical_not(is_cell), jnp.logical_and(step > 0, step < ITERS)))
        def _():
            newton_step(False)

    keep = table[0, 2 * CHIPS] != 0
    owned_ref[...] = jnp.where(keep, x_ref[...], jnp.zeros(x_ref.shape, x_ref.dtype))

    @pl.loop(0, CHIPS // 2)
    def _(i):
        unit = cells.at[0]
        pltpu.make_async_copy(unit, unit, up_recv.at[2 * i + 1]).wait()
        pltpu.make_async_copy(unit, unit, down_recv.at[2 * i]).wait()

    plane_cells = cells.at[pl.ds(0, CHIPS)]
    pltpu.make_async_copy(plane_cells, plane_cells, far_recv).wait()

    most = staged.at[pl.ds(0, OWNERS - 1)]
    pltpu.make_async_copy(most, most, send_sem).wait()

    @pl.when(is_cell)
    def _():
        pltpu.make_async_copy(most, most, back_send).wait()

    sent = cells.at[pl.ds(0, 3 * CHIPS)]
    pltpu.make_async_copy(sent, sent, rep_send).wait()


def finish(table, new_ref, cells, owned_ref, new_out, update_out, owned_out, sem):
    new_copy = pltpu.make_async_copy(new_ref, new_out, sem.at[0])
    owned_copy = pltpu.make_async_copy(owned_ref, owned_out, sem.at[1])
    new_copy.start()

    @pl.loop(0, MATS, unroll=8)
    def _(m):
        pltpu.make_async_copy(cells.at[table[1, m]], update_out.at[m], sem.at[2]).start()

    owned_copy.start()
    pltpu.make_async_copy(cells, update_out, sem.at[2]).wait()
    new_copy.wait()
    owned_copy.wait()


def local(grad, momentum, owner_list):
    mats, rows, cols = grad.shape
    vmem = pl.BlockSpec(memory_space=pltpu.VMEM)
    smem = pl.BlockSpec(memory_space=pltpu.SMEM)
    hbm = pl.BlockSpec(memory_space=pltpu.HBM)
    pin = pltpu.with_memory_space_constraint
    hold = pl.BlockSpec(memory_space=pl.ANY)
    dma = pltpu.SemaphoreType.DMA
    outs = (
        jax.ShapeDtypeStruct(momentum.shape, jnp.float32),
        jax.ShapeDtypeStruct(grad.shape, jnp.bfloat16),
        jax.ShapeDtypeStruct((rows * OWNERS, cols), jnp.bfloat16),
    )
    new_momentum, cells, owned, table = pl.pallas_call(
        kernel,
        out_shape=(*(pltpu.VMEM(o.shape, o.dtype) for o in outs), pltpu.VMEM((2, MATS), jnp.int32)),
        in_specs=[vmem, hbm, hbm],
        out_specs=(vmem, vmem, vmem, vmem),
        scratch_shapes=[
            pltpu.VMEM((mats, rows, cols), jnp.bfloat16),
            pltpu.VMEM((mats, rows, cols), jnp.float32),
            pltpu.VMEM((OWNERS, rows, cols), jnp.bfloat16),
            pltpu.VMEM((rows * OWNERS, cols), jnp.bfloat16),
            pltpu.SMEM((2, MATS), jnp.int32),
            dma((3,)),
            dma,
            dma,
            dma((1,)),
            dma,
            dma((CHIPS,)),
            dma,
            dma((CHIPS,)),
            dma((CHIPS,)),
            dma,
        ],
        compiler_params=pltpu.CompilerParams(
            collective_id=0, has_side_effects=True, vmem_limit_bytes=40 * 1024 * 1024
        ),
        name="muon",
    )(owner_list.reshape(1, MATS), pin(grad, pltpu.HBM), pin(momentum, pltpu.HBM))
    new_momentum, update, owned = pl.pallas_call(
        finish,
        out_shape=outs,
        in_specs=[smem, hold, hold, hold],
        out_specs=(hbm, hbm, hbm),
        scratch_shapes=[dma((3,))],
        compiler_params=pltpu.CompilerParams(vmem_limit_bytes=1024 * 1024),
        name="finish",
    )(table, new_momentum, cells, owned)
    return new_momentum, update, owned[None]


def solution(mesh):
    in_specs = (P(None, "fsdp", None), P(None, "fsdp", None), P())
    out_specs = (P(None, "fsdp", None), P(None, "fsdp", None), P(("fsdp", "rep"), None, None))
    return jax.shard_map(local, mesh=mesh, in_specs=in_specs, out_specs=out_specs, check_vma=False)
```

```python
import functools

import jax
import jax.numpy as jnp
from jax import lax
from jax.experimental import pallas as pl
from jax.experimental.pallas import tpu as pltpu
from jax.sharding import PartitionSpec as P

ITERS = 5
decay_rate = 0.95
norm_eps = 1e-07
quintic_a = 3.4445
quintic_b = -4.775
quintic_c = 2.0315

MESH = pl.DeviceIdType.MESH
NX, NZ, NY = 4, 8, 4
CHIPS = NX * NZ
OWNERS = 2 * CHIPS
MATS = 128
HALF = CHIPS // 2
BLOCK = 4
BLOCKS = CHIPS // BLOCK
LAG = 2
ORDER = (0, 1, 4, 2, 5, 3, 6, 7)
STEP_AT = (7, 8, 9, 9, 9)
WIDTH = 256


def routing(owner_row, table, plane, me, px, pz):
    square = (MATS, MATS)
    down = lax.broadcasted_iota(jnp.int32, square, 0)
    along = lax.broadcasted_iota(jnp.int32, square, 1)
    owner_r = jnp.broadcast_to(owner_row, square)
    owner_c = owner_r.T
    same = jnp.where(owner_r == owner_c, 1, 0)
    slot_r = jnp.sum(jnp.where(down < along, same, 0), axis=0, keepdims=True)
    slot_c = jnp.sum(jnp.where(along < down, same, 0), axis=1, keepdims=True)
    code_r = owner_r * 4 + slot_r
    code_c = owner_c * 4 + slot_c

    def cell_code(q):
        slot = q // CHIPS
        return ((q % CHIPS) * 2 + slot // 2) * 4 + slot

    def spare(owner, slot):
        return jnp.where((slot // 2) == (owner % 2), 0, 1)

    spare_r = spare(owner_r, slot_r)
    spare_c = spare(owner_c, slot_c)
    match = jnp.where(code_r == cell_code(down), 1, 0)
    empty_c = 1 - jnp.max(match, axis=1, keepdims=True)
    empty_r = 1 - jnp.max(jnp.where(code_c == cell_code(along), 1, 0), axis=0, keepdims=True)
    spare_rank = jnp.sum(jnp.where(down < along, spare_c, 0), axis=0, keepdims=True)
    empty_rank = jnp.sum(jnp.where(along < down, jnp.broadcast_to(empty_r, square), 0), axis=1, keepdims=True)
    stand_in = jnp.where(spare_rank == empty_rank, spare_r * empty_c, 0)
    cell_of = jnp.sum((match + stand_in) * down, axis=0, keepdims=True)
    cell_of_c = jnp.broadcast_to(cell_of, square).T
    other = ((along - CHIPS) * 2 + 1 - plane // 2) * 4 + plane
    wanted = jnp.where(along < 2 * CHIPS, other, me * 4 + plane)
    hit = jnp.where(along < CHIPS, cell_of_c - plane * CHIPS - along, code_c - wanted) == 0
    number = jnp.where(along < 2 * CHIPS, down, 1)
    table[0:1, :] = jnp.clip(jnp.sum(jnp.where(hit, number, 0), axis=0, keepdims=True), 0, MATS - 1)
    chip = down % CHIPS
    x, z = chip // NZ, chip % NZ
    place = (down // CHIPS) * CHIPS + (x + z) % 2 * HALF + (px + NX - x) % NX * BLOCK + (pz + NZ - z) % NZ // 2
    place = jnp.sum((match + stand_in) * place, axis=0, keepdims=True)
    table[1:2, :] = jnp.clip(place, 0, MATS - 1)


def kernel(owner_hbm, grad_hbm, momentum_hbm, new_ref, cells, owned_ref, table_ref, owner, grad, momentum, staged, x_ref,
           gram_ref, table, in_sem, send_sem, recv_sem, self_sem, back_send, back_recv, rep_send, up_recv, down_recv,
           far_recv):
    f = lax.axis_index("fsdp")
    y = lax.axis_index("rep")
    chip = f // 2
    core = f % 2
    px = chip // NZ
    pz = chip % NZ
    parity = lax.rem(px + pz, 2)
    cell_core = y // 2
    is_cell = core == cell_core
    no_cell = jnp.logical_not(is_cell)

    load_owner = pltpu.make_async_copy(owner_hbm, owner, in_sem.at[3])
    load_grad = pltpu.make_async_copy(grad_hbm, grad, in_sem.at[0])
    load_momentum = pltpu.make_async_copy(momentum_hbm, momentum, in_sem.at[1])
    load_owner.start()
    load_grad.start()
    load_momentum.start()

    barrier = pltpu.get_barrier_semaphore()

    @pl.loop(1, OWNERS)
    def _(k):
        pl.semaphore_signal(barrier, inc=1, device_id={"fsdp": lax.rem(f + k, OWNERS)}, device_id_type=MESH)

    for k in range(1, NY):
        pl.semaphore_signal(barrier, inc=1, device_id={"rep": lax.rem(y + k, NY)}, device_id_type=MESH)
    load_owner.wait()
    routing(owner[...], table_ref, y, f, px, pz)
    load_table = pltpu.make_async_copy(table_ref, table, in_sem.at[2])
    load_table.start()
    load_table.wait()
    load_grad.wait()
    load_momentum.wait()
    pl.semaphore_wait(barrier, OWNERS - 1 + NY - 1)

    def stage(there, part):
        which = table[0, part * CHIPS + there]
        g = grad[which].astype(jnp.float32)
        blended = g + decay_rate * (decay_rate * momentum[which] + g)
        staged[part * CHIPS + there] = blended.astype(jnp.bfloat16)

    def send(there, part, to):
        rows = staged.at[part * CHIPS + there]
        target = x_ref.at[pl.ds(f * 4, 4)]

        @pl.when(to == f)
        def _():
            pltpu.make_async_copy(rows, target, self_sem.at[0]).start()

        @pl.when(to != f)
        def _():
            pltpu.make_async_remote_copy(
                src_ref=rows,
                dst_ref=target,
                send_sem=send_sem,
                recv_sem=recv_sem,
                device_id={"fsdp": to},
                device_id_type=MESH,
            ).start()

    def each(batch, action):
        @pl.loop(0, HALF)
        def _(i):
            dx = i // 4
            dz = 2 * lax.rem(i, 4) + lax.rem(dx + parity + batch, 2)
            action(lax.rem(px + dx, NX) * NZ + lax.rem(pz + dz, NZ))

    def forward(there):
        stage(there, 0)
        send(there, 0, there * 2 + cell_core)

    def other(there):
        stage(there, 1)
        send(there, 1, there * 2 + 1 - cell_core)

    for batch in range(2):
        each(batch, forward)

    @pl.when(no_cell)
    def _():
        for batch in range(2):
            each(batch, other)

    @pl.loop(0, MATS)
    def _(m):
        new_ref[m] = decay_rate * momentum[m] + grad[m].astype(jnp.float32)

    def receive():
        pltpu.make_async_copy(staged.at[0], x_ref.at[pl.ds(f * 4, 4)], self_sem.at[0]).wait()
        half = staged.at[pl.ds(0, OWNERS - 1)]
        pltpu.make_async_copy(half, half, recv_sem).wait()

    def gram_of(x):
        return lax.dot_general(x, x, (((1,), (1,)), ((), ())), preferred_element_type=jnp.float32)

    def newton_step(first, last):
        if first:
            gram = gram_of(x_ref[...])
            row = lax.broadcasted_iota(jnp.int32, gram.shape, 0)
            col = lax.broadcasted_iota(jnp.int32, gram.shape, 1)
            total = jnp.sum(jnp.where(row == col, gram, 0.0), axis=(0, 1), keepdims=True)
            scale = 1.0 / (jnp.sqrt(total) + norm_eps)
            gram = gram * (scale * scale)
        else:
            gram = gram_ref[...]
        low = gram.astype(jnp.bfloat16)
        square = jnp.dot(low, low, preferred_element_type=jnp.float32)
        poly = (quintic_b * low.astype(jnp.float32) + quintic_c * square).astype(jnp.bfloat16)
        gram = None
        for c in range(x_ref.shape[1] // WIDTH):
            cols = pl.ds(c * WIDTH, WIDTH)
            x = x_ref[:, cols]
            result = quintic_a * x.astype(jnp.float32) + jnp.dot(poly, x, preferred_element_type=jnp.float32)
            if first:
                result = result * scale
            result = result.astype(jnp.bfloat16)
            x_ref[:, cols] = result
            if not last:
                gram = gram_of(result) if gram is None else gram + gram_of(result)
        if not last:
            gram_ref[...] = gram

    @pl.when(is_cell)
    def _():
        receive()
        for step in range(ITERS):
            newton_step(step == 0, step == ITERS - 1)
        base = y * CHIPS + parity * HALF

        @pl.loop(0, CHIPS)
        def _(j):
            dx = j // NZ
            dz = lax.rem(j, NZ)
            there = lax.rem(px + dx, NX) * NZ + lax.rem(pz + dz, NZ)
            target = cells.at[base + dx * BLOCK + dz // 2]
            arrived = back_recv.at[parity * NX + dx]
            for to_core in range(2):
                to = there * 2 + to_core
                rows = x_ref.at[pl.ds(to * 4, 4)]

                @pl.when(to == f)
                def _():
                    pltpu.make_async_copy(rows, target, arrived).start()

                @pl.when(to != f)
                def _():
                    pltpu.make_async_remote_copy(
                        src_ref=rows,
                        dst_ref=target,
                        send_sem=back_send,
                        recv_sem=arrived,
                        device_id={"fsdp": to},
                        device_id_type=MESH,
                    ).start()

        for batch in range(2):
            each(batch, other)

    up = lax.rem(y + 1, NY)
    below = lax.rem(y + NY - 1, NY)

    def block_of(plane, b):
        return cells.at[pl.ds(plane * CHIPS + b * BLOCK, BLOCK)]

    def arrive(plane, b, sem):
        pltpu.make_async_copy(block_of(plane, b), block_of(plane, b), sem).wait()

    def pass_on(plane, b, to, sem):
        pltpu.make_async_remote_copy(
            src_ref=block_of(plane, b),
            dst_ref=block_of(plane, b),
            send_sem=rep_send,
            recv_sem=sem,
            device_id={"rep": to},
            device_id_type=MESH,
        ).start()

    for at in range(BLOCKS + LAG):
        if at < BLOCKS:
            b = ORDER[at]
            arrive(y, b, back_recv.at[b])
            pass_on(y, b, up, up_recv.at[b])
            pass_on(y, b, below, down_recv.at[b])
        if at >= LAG:
            b = ORDER[at - LAG]
            if b % 2 == 0:
                arrive(below, b, up_recv.at[b])
                pass_on(below, b, up, far_recv)
            else:
                arrive(up, b, down_recv.at[b])
                pass_on(up, b, below, far_recv)
        for step in range(ITERS):
            if STEP_AT[step] == at:

                @pl.when(no_cell)
                def _():
                    if step == 0:
                        receive()
                    newton_step(step == 0, step == ITERS - 1)

    keep = table[0, 2 * CHIPS] != 0
    owned_ref[...] = jnp.where(keep, x_ref[...], jnp.zeros(x_ref.shape, x_ref.dtype))

    for b in range(0, BLOCKS, 2):
        arrive(up, b, down_recv.at[b])
        arrive(below, b + 1, up_recv.at[b + 1])
    plane_cells = cells.at[pl.ds(0, CHIPS)]
    pltpu.make_async_copy(plane_cells, plane_cells, far_recv).wait()

    most = staged.at[pl.ds(0, OWNERS - 1)]
    pltpu.make_async_copy(most, most, send_sem).wait()

    @pl.when(is_cell)
    def _():
        pltpu.make_async_copy(most, most, back_send).wait()

    sent = cells.at[pl.ds(0, 3 * CHIPS)]
    pltpu.make_async_copy(sent, sent, rep_send).wait()


def finish(table, new_ref, cells, owned_ref, new_out, update_out, owned_out, sem):
    new_copy = pltpu.make_async_copy(new_ref, new_out, sem.at[0])
    owned_copy = pltpu.make_async_copy(owned_ref, owned_out, sem.at[1])
    new_copy.start()

    @pl.loop(0, MATS, unroll=8)
    def _(m):
        pltpu.make_async_copy(cells.at[table[1, m]], update_out.at[m], sem.at[2]).start()

    owned_copy.start()
    pltpu.make_async_copy(cells, update_out, sem.at[2]).wait()
    new_copy.wait()
    owned_copy.wait()


def local(grad, momentum, owner_list):
    mats, rows, cols = grad.shape
    vmem = pl.BlockSpec(memory_space=pltpu.VMEM)
    smem = pl.BlockSpec(memory_space=pltpu.SMEM)
    hbm = pl.BlockSpec(memory_space=pltpu.HBM)
    pin = pltpu.with_memory_space_constraint
    hold = pl.BlockSpec(memory_space=pl.ANY)
    dma = pltpu.SemaphoreType.DMA
    outs = (
        jax.ShapeDtypeStruct(momentum.shape, jnp.float32),
        jax.ShapeDtypeStruct(grad.shape, jnp.bfloat16),
        jax.ShapeDtypeStruct((rows * OWNERS, cols), jnp.bfloat16),
    )
    new_momentum, cells, owned, table = pl.pallas_call(
        kernel,
        out_shape=(*(pltpu.VMEM(o.shape, o.dtype) for o in outs), pltpu.VMEM((2, MATS), jnp.int32)),
        in_specs=[hbm, hbm, hbm],
        out_specs=(vmem, vmem, vmem, vmem),
        scratch_shapes=[
            pltpu.VMEM((1, MATS), jnp.int32),
            pltpu.VMEM((mats, rows, cols), jnp.bfloat16),
            pltpu.VMEM((mats, rows, cols), jnp.float32),
            pltpu.VMEM((OWNERS, rows, cols), jnp.bfloat16),
            pltpu.VMEM((rows * OWNERS, cols), jnp.bfloat16),
            pltpu.VMEM((rows * OWNERS, rows * OWNERS), jnp.float32),
            pltpu.SMEM((2, MATS), jnp.int32),
            dma((4,)),
            dma,
            dma,
            dma((1,)),
            dma,
            dma((BLOCKS,)),
            dma,
            dma((BLOCKS,)),
            dma((BLOCKS,)),
            dma,
        ],
        compiler_params=pltpu.CompilerParams(
            collective_id=0, has_side_effects=True, vmem_limit_bytes=40 * 1024 * 1024
        ),
        name="muon",
    )(pin(owner_list.reshape(1, MATS), pltpu.HBM), pin(grad, pltpu.HBM), pin(momentum, pltpu.HBM))
    new_momentum, update, owned = pl.pallas_call(
        finish,
        out_shape=outs,
        in_specs=[smem, hold, hold, hold],
        out_specs=(hbm, hbm, hbm),
        scratch_shapes=[dma((3,))],
        compiler_params=pltpu.CompilerParams(vmem_limit_bytes=1024 * 1024),
        name="finish",
    )(table, new_momentum, cells, owned)
    return new_momentum, update, owned[None]


def solution(mesh):
    in_specs = (P(None, "fsdp", None), P(None, "fsdp", None), P())
    out_specs = (P(None, "fsdp", None), P(None, "fsdp", None), P(("fsdp", "rep"), None, None))
    return jax.shard_map(local, mesh=mesh, in_specs=in_specs, out_specs=out_specs, check_vma=False)
```

```python
import functools

import jax
import jax.numpy as jnp
from jax import lax
from jax.experimental import pallas as pl
from jax.experimental.pallas import tpu as pltpu
from jax.sharding import PartitionSpec as P

ITERS = 5
decay_rate = 0.95
norm_eps = 1e-07
quintic_a = 3.4445
quintic_b = -4.775
quintic_c = 2.0315

MESH = pl.DeviceIdType.MESH
NX, NZ, NY = 4, 8, 4
CHIPS = NX * NZ
OWNERS = 2 * CHIPS
MATS = 128
HALF = CHIPS // 2
BLOCK = 4
BLOCKS = CHIPS // BLOCK
LAG = 1
ORDER = (0, 1, 4, 2, 5, 3, 6, 7)
STEP_AT = (7, 8, 8, 8, 8)
WIDTH = 256


def routing(owner_row, table, plane, me, px, pz):
    square = (MATS, MATS)
    down = lax.broadcasted_iota(jnp.int32, square, 0)
    along = lax.broadcasted_iota(jnp.int32, square, 1)
    owner_r = jnp.broadcast_to(owner_row, square)
    owner_c = owner_r.T
    same = jnp.where(owner_r == owner_c, 1, 0)
    slot_r = jnp.sum(jnp.where(down < along, same, 0), axis=0, keepdims=True)
    slot_c = jnp.sum(jnp.where(along < down, same, 0), axis=1, keepdims=True)
    code_r = owner_r * 4 + slot_r
    code_c = owner_c * 4 + slot_c

    def cell_code(q):
        slot = q // CHIPS
        return ((q % CHIPS) * 2 + slot // 2) * 4 + slot

    def spare(owner, slot):
        return jnp.where((slot // 2) == (owner % 2), 0, 1)

    spare_r = spare(owner_r, slot_r)
    spare_c = spare(owner_c, slot_c)
    match = jnp.where(code_r == cell_code(down), 1, 0)
    empty_c = 1 - jnp.max(match, axis=1, keepdims=True)
    empty_r = 1 - jnp.max(jnp.where(code_c == cell_code(along), 1, 0), axis=0, keepdims=True)
    spare_rank = jnp.sum(jnp.where(down < along, spare_c, 0), axis=0, keepdims=True)
    empty_rank = jnp.sum(jnp.where(along < down, jnp.broadcast_to(empty_r, square), 0), axis=1, keepdims=True)
    stand_in = jnp.where(spare_rank == empty_rank, spare_r * empty_c, 0)
    cell_of = jnp.sum((match + stand_in) * down, axis=0, keepdims=True)
    cell_of_c = jnp.broadcast_to(cell_of, square).T
    other = ((along - CHIPS) * 2 + 1 - plane // 2) * 4 + plane
    wanted = jnp.where(along < 2 * CHIPS, other, me * 4 + plane)
    hit = jnp.where(along < CHIPS, cell_of_c - plane * CHIPS - along, code_c - wanted) == 0
    number = jnp.where(along < 2 * CHIPS, down, 1)
    table[0:1, :] = jnp.clip(jnp.sum(jnp.where(hit, number, 0), axis=0, keepdims=True), 0, MATS - 1)
    chip = down % CHIPS
    x, z = chip // NZ, chip % NZ
    place = (down // CHIPS) * CHIPS + (x + z) % 2 * HALF + (px + NX - x) % NX * BLOCK + (pz + NZ - z) % NZ // 2
    place = jnp.sum((match + stand_in) * place, axis=0, keepdims=True)
    table[1:2, :] = jnp.clip(place, 0, MATS - 1)


def kernel(owner_hbm, grad_hbm, momentum_hbm, new_ref, cells, owned_ref, table_ref, owner, grad, momentum, staged, x_ref,
           gram_ref, table, in_sem, send_sem, recv_sem, self_sem, back_send, back_recv, rep_send, up_recv, down_recv,
           far_recv):
    f = lax.axis_index("fsdp")
    y = lax.axis_index("rep")
    chip = f // 2
    core = f % 2
    px = chip // NZ
    pz = chip % NZ
    parity = lax.rem(px + pz, 2)
    cell_core = y // 2
    is_cell = core == cell_core
    no_cell = jnp.logical_not(is_cell)

    load_owner = pltpu.make_async_copy(owner_hbm, owner, in_sem.at[3])
    load_grad = pltpu.make_async_copy(grad_hbm, grad, in_sem.at[0])
    load_momentum = pltpu.make_async_copy(momentum_hbm, momentum, in_sem.at[1])
    load_owner.start()
    load_grad.start()
    load_momentum.start()

    barrier = pltpu.get_barrier_semaphore()

    @pl.loop(1, OWNERS, unroll=21)
    def _(k):
        pl.semaphore_signal(barrier, inc=1, device_id={"fsdp": lax.rem(f + k, OWNERS)}, device_id_type=MESH)

    for k in range(1, NY):
        pl.semaphore_signal(barrier, inc=1, device_id={"rep": lax.rem(y + k, NY)}, device_id_type=MESH)
    load_owner.wait()
    routing(owner[...], table_ref, y, f, px, pz)
    load_table = pltpu.make_async_copy(table_ref, table, in_sem.at[2])
    load_table.start()
    load_table.wait()
    load_grad.wait()
    load_momentum.wait()
    pl.semaphore_wait(barrier, OWNERS - 1 + NY - 1)

    def stage(there, part):
        which = table[0, part * CHIPS + there]
        g = grad[which].astype(jnp.float32)
        blended = g + decay_rate * (decay_rate * momentum[which] + g)
        staged[part * CHIPS + there] = blended.astype(jnp.bfloat16)

    def send(there, part, to):
        rows = staged.at[part * CHIPS + there]
        target = x_ref.at[pl.ds(f * 4, 4)]

        @pl.when(to == f)
        def _():
            pltpu.make_async_copy(rows, target, self_sem.at[0]).start()

        @pl.when(to != f)
        def _():
            pltpu.make_async_remote_copy(
                src_ref=rows,
                dst_ref=target,
                send_sem=send_sem,
                recv_sem=recv_sem,
                device_id={"fsdp": to},
                device_id_type=MESH,
            ).start()

    def each(batch, action):
        @pl.loop(0, HALF)
        def _(i):
            dx = i // 4
            dz = 2 * lax.rem(i, 4) + lax.rem(dx + parity + batch, 2)
            action(lax.rem(px + dx, NX) * NZ + lax.rem(pz + dz, NZ))

    def forward(there):
        stage(there, 0)
        send(there, 0, there * 2 + cell_core)

    def other(there):
        stage(there, 1)
        send(there, 1, there * 2 + 1 - cell_core)

    for batch in range(2):
        each(batch, forward)

    @pl.when(no_cell)
    def _():
        for batch in range(2):
            each(batch, other)

    @pl.loop(0, MATS)
    def _(m):
        new_ref[m] = decay_rate * momentum[m] + grad[m].astype(jnp.float32)

    def receive():
        pltpu.make_async_copy(staged.at[0], x_ref.at[pl.ds(f * 4, 4)], self_sem.at[0]).wait()
        half = staged.at[pl.ds(0, OWNERS - 1)]
        pltpu.make_async_copy(half, half, recv_sem).wait()

    def gram_of(x):
        return lax.dot_general(x, x, (((1,), (1,)), ((), ())), preferred_element_type=jnp.float32)

    def newton_step(first, last):
        if first:
            gram = gram_of(x_ref[...])
            row = lax.broadcasted_iota(jnp.int32, gram.shape, 0)
            col = lax.broadcasted_iota(jnp.int32, gram.shape, 1)
            total = jnp.sum(jnp.where(row == col, gram, 0.0), axis=(0, 1), keepdims=True)
            scale = 1.0 / (jnp.sqrt(total) + norm_eps)
            gram = gram * (scale * scale)
        else:
            gram = gram_ref[...]
        low = gram.astype(jnp.bfloat16)
        square = jnp.dot(low, low, preferred_element_type=jnp.float32)
        poly = (quintic_b * low.astype(jnp.float32) + quintic_c * square).astype(jnp.bfloat16)
        gram = None
        for c in range(x_ref.shape[1] // WIDTH):
            cols = pl.ds(c * WIDTH, WIDTH)
            x = x_ref[:, cols]
            result = quintic_a * x.astype(jnp.float32) + jnp.dot(poly, x, preferred_element_type=jnp.float32)
            if first:
                result = result * scale
            result = result.astype(jnp.bfloat16)
            x_ref[:, cols] = result
            if not last:
                gram = gram_of(result) if gram is None else gram + gram_of(result)
        if not last:
            gram_ref[...] = gram

    @pl.when(is_cell)
    def _():
        receive()
        for step in range(ITERS):
            newton_step(step == 0, step == ITERS - 1)
        base = y * CHIPS + parity * HALF

        @pl.loop(0, CHIPS)
        def _(j):
            dx = j // NZ
            dz = lax.rem(j, NZ)
            there = lax.rem(px + dx, NX) * NZ + lax.rem(pz + dz, NZ)
            target = cells.at[base + dx * BLOCK + dz // 2]
            arrived = back_recv.at[parity * NX + dx]
            for to_core in range(2):
                to = there * 2 + to_core
                rows = x_ref.at[pl.ds(to * 4, 4)]

                @pl.when(to == f)
                def _():
                    pltpu.make_async_copy(rows, target, arrived).start()

                @pl.when(to != f)
                def _():
                    pltpu.make_async_remote_copy(
                        src_ref=rows,
                        dst_ref=target,
                        send_sem=back_send,
                        recv_sem=arrived,
                        device_id={"fsdp": to},
                        device_id_type=MESH,
                    ).start()

        for batch in range(2):
            each(batch, other)

    up = lax.rem(y + 1, NY)
    below = lax.rem(y + NY - 1, NY)

    def block_of(plane, b):
        return cells.at[pl.ds(plane * CHIPS + b * BLOCK, BLOCK)]

    def arrive(plane, b, sem):
        pltpu.make_async_copy(block_of(plane, b), block_of(plane, b), sem).wait()

    def pass_on(plane, b, to, sem):
        pltpu.make_async_remote_copy(
            src_ref=block_of(plane, b),
            dst_ref=block_of(plane, b),
            send_sem=rep_send,
            recv_sem=sem,
            device_id={"rep": to},
            device_id_type=MESH,
        ).start()

    for at in range(BLOCKS + LAG):
        if at < BLOCKS:
            b = ORDER[at]
            arrive(y, b, back_recv.at[b])
            pass_on(y, b, up, up_recv.at[b])
            pass_on(y, b, below, down_recv.at[b])
        if at >= LAG:
            b = ORDER[at - LAG]
            if b % 2 == 0:
                arrive(below, b, up_recv.at[b])
                pass_on(below, b, up, far_recv)
            else:
                arrive(up, b, down_recv.at[b])
                pass_on(up, b, below, far_recv)
        for step in range(ITERS):
            if STEP_AT[step] == at:

                @pl.when(no_cell)
                def _():
                    if step == 0:
                        receive()
                    newton_step(step == 0, step == ITERS - 1)

    keep = table[0, 2 * CHIPS] != 0
    owned_ref[...] = jnp.where(keep, x_ref[...], jnp.zeros(x_ref.shape, x_ref.dtype))

    for b in range(0, BLOCKS, 2):
        arrive(up, b, down_recv.at[b])
        arrive(below, b + 1, up_recv.at[b + 1])
    plane_cells = cells.at[pl.ds(0, CHIPS)]
    pltpu.make_async_copy(plane_cells, plane_cells, far_recv).wait()

    most = staged.at[pl.ds(0, OWNERS - 1)]
    pltpu.make_async_copy(most, most, send_sem).wait()

    @pl.when(is_cell)
    def _():
        pltpu.make_async_copy(most, most, back_send).wait()

    sent = cells.at[pl.ds(0, 3 * CHIPS)]
    pltpu.make_async_copy(sent, sent, rep_send).wait()


def finish(table, new_ref, cells, owned_ref, new_out, update_out, owned_out, sem):
    new_copy = pltpu.make_async_copy(new_ref, new_out, sem.at[0])
    owned_copy = pltpu.make_async_copy(owned_ref, owned_out, sem.at[1])
    new_copy.start()

    @pl.loop(0, MATS, unroll=8)
    def _(m):
        pltpu.make_async_copy(cells.at[table[1, m]], update_out.at[m], sem.at[2]).start()

    owned_copy.start()
    pltpu.make_async_copy(cells, update_out, sem.at[2]).wait()
    new_copy.wait()
    owned_copy.wait()


def local(grad, momentum, owner_list):
    mats, rows, cols = grad.shape
    vmem = pl.BlockSpec(memory_space=pltpu.VMEM)
    smem = pl.BlockSpec(memory_space=pltpu.SMEM)
    hbm = pl.BlockSpec(memory_space=pltpu.HBM)
    pin = pltpu.with_memory_space_constraint
    hold = pl.BlockSpec(memory_space=pl.ANY)
    dma = pltpu.SemaphoreType.DMA
    outs = (
        jax.ShapeDtypeStruct(momentum.shape, jnp.float32),
        jax.ShapeDtypeStruct(grad.shape, jnp.bfloat16),
        jax.ShapeDtypeStruct((rows * OWNERS, cols), jnp.bfloat16),
    )
    new_momentum, cells, owned, table = pl.pallas_call(
        kernel,
        out_shape=(*(pltpu.VMEM(o.shape, o.dtype) for o in outs), pltpu.VMEM((2, MATS), jnp.int32)),
        in_specs=[hbm, hbm, hbm],
        out_specs=(vmem, vmem, vmem, vmem),
        scratch_shapes=[
            pltpu.VMEM((1, MATS), jnp.int32),
            pltpu.VMEM((mats, rows, cols), jnp.bfloat16),
            pltpu.VMEM((mats, rows, cols), jnp.float32),
            pltpu.VMEM((OWNERS, rows, cols), jnp.bfloat16),
            pltpu.VMEM((rows * OWNERS, cols), jnp.bfloat16),
            pltpu.VMEM((rows * OWNERS, rows * OWNERS), jnp.float32),
            pltpu.SMEM((2, MATS), jnp.int32),
            dma((4,)),
            dma,
            dma,
            dma((1,)),
            dma,
            dma((BLOCKS,)),
            dma,
            dma((BLOCKS,)),
            dma((BLOCKS,)),
            dma,
        ],
        compiler_params=pltpu.CompilerParams(
            collective_id=0, has_side_effects=True, vmem_limit_bytes=40 * 1024 * 1024
        ),
        name="muon",
    )(pin(owner_list.reshape(1, MATS), pltpu.HBM), pin(grad, pltpu.HBM), pin(momentum, pltpu.HBM))
    new_momentum, update, owned = pl.pallas_call(
        finish,
        out_shape=outs,
        in_specs=[smem, hold, hold, hold],
        out_specs=(hbm, hbm, hbm),
        scratch_shapes=[dma((3,))],
        compiler_params=pltpu.CompilerParams(vmem_limit_bytes=1024 * 1024),
        name="finish",
    )(table, new_momentum, cells, owned)
    return new_momentum, update, owned[None]


def solution(mesh):
    in_specs = (P(None, "fsdp", None), P(None, "fsdp", None), P())
    out_specs = (P(None, "fsdp", None), P(None, "fsdp", None), P(("fsdp", "rep"), None, None))
    return jax.shard_map(local, mesh=mesh, in_specs=in_specs, out_specs=out_specs, check_vma=False)
```
